32 devices in a mesh: energy: 8 (over z, core), momentum: 4 (over y, x).
Axes of the slice: x: 2, y: 2, z: 4, core: 2. Of those that a mesh axis runs over, the one named last changes fastest.
Arguments:
- green_ret: bfloat16 [16, 8, 2, 512, 512], P('energy', 'momentum'), may hold values from -0.1875 to 0.1875
- sigma_in: bfloat16 [16, 8, 2, 512, 512], P('energy', 'momentum'), may hold values from -6 to 6
- screened: bfloat16 [32, 16, 8, 2, 8192], P(('energy', 'momentum')), may hold values from -6 to 6
- block_of_slot: int32 [32], replicated, may hold values from 0 to 31, each once
Outputs:
- green_new: bfloat16 [16, 8, 2, 512, 512], P('energy', 'momentum')
The draws below stay inside these ranges and needn't reach their ends.
Inputs may be any that keep to these rules, and one draw needn't show every extreme that they name: block_of_slot is a permutation of the blocks 0 to 31.
All inputs are finite; a program needn't handle non-finite values.
Results may differ from the reference program's by a relative error of at most 0.0085.
Values may be sent and summed in bfloat16 or wider, within the bound.
No kernel may reach another device: no remote copies, remote signals or barrier semaphores. Data moves between devices by JAX's collectives and lax.ppermute only.
A program may use at most 128 MiB of HBM per device.

```python
import jax
import jax.numpy as jnp
from jax import lax

NO = 512
NE = 16
NK = 8
NBLK = 32
PB = 8192


def shard_levels(own_key, shape, cuts, least, top_value):
    gain, own = 1.0, jax.random.fold_in(own_key, 6)
    for axis_at, parts in cuts:
        steps = jnp.exp(jax.random.uniform(jax.random.fold_in(own, axis_at), (parts,), jnp.float32, least / len(cuts), top_value / len(cuts)))
        gain = gain * jnp.repeat(steps, shape[axis_at] // parts).reshape([-1 if axis == axis_at else 1 for axis in range(len(shape))])
    return gain


def normal_values(rng, shape, width, most, shards=(), dtype=jnp.bfloat16):
    values = width * jax.random.normal(rng, shape, jnp.float32)
    if shards:
        values = values * shard_levels(rng, shape, shards, -0.22, 0.18)
    return jnp.clip(values, -most, most).astype(dtype)


def setup_inputs(seed: int = 0) -> dict:
    streams_of = jax.random.split(jax.random.key(seed), 5)
    green_ret = normal_values(streams_of[0], (NE, NK, 2, NO, NO), (2 * NO) ** -0.5, 0.1875, ((0, 8), (1, 4)))
    sigma_in = normal_values(streams_of[1], (NE, NK, 2, NO, NO), 1.0, 6.0, ((0, 8), (1, 4)))
    screened = normal_values(streams_of[2], (NBLK, NE, NK, 2, PB), 0.7, 6.0, ((0, 32),))
    block_of_slot = jax.random.permutation(streams_of[3], NBLK).astype(jnp.int32)
    return {"green_ret": green_ret, "sigma_in": sigma_in, "screened": screened, "block_of_slot": block_of_slot}


def matmul(left_side, right_side):
    return jnp.dot(left_side, right_side, preferred_element_type=jnp.float32)


def sandwich(green, sigma):
    green_real = green[0]
    green_imag = green[1]
    sigma_real = sigma[0]
    sigma_imag = sigma[1]
    first_real = (matmul(green_real, sigma_real) - matmul(green_imag, sigma_imag)).astype(jnp.bfloat16)
    first_imag = (matmul(green_real, sigma_imag) + matmul(green_imag, sigma_real)).astype(jnp.bfloat16)
    second_real = matmul(first_real, green_real.T) + matmul(first_imag, green_imag.T)
    second_imag = matmul(first_imag, green_real.T) - matmul(first_real, green_imag.T)
    return jnp.stack([second_real, second_imag]).astype(jnp.bfloat16)


def sandwich_all(green, sigma):
    flat_green = green.reshape(NE * NK, 2, NO, NO)
    flat_sigma = sigma.reshape(NE * NK, 2, NO, NO)
    result = lax.map(lambda both: sandwich(both[0], both[1]), (flat_green, flat_sigma))
    return result.reshape(NE, NK, 2, NO, NO)


def reference(green_ret, sigma_in, screened, block_of_slot):
    green = sandwich_all(green_ret, sigma_in)
    blocks = green.reshape(NE, NK, 2, NBLK, PB)

    def convolve_slot(both):
        block_index, weight = both
        piece = lax.dynamic_index_in_dim(blocks, block_index, axis=3, keepdims=False).astype(jnp.float32)
        values = lax.complex(piece[:, :, 0], piece[:, :, 1])
        spectrum = jnp.fft.fft2(values, axes=(0, 1))
        factor = lax.complex(weight[:, :, 0].astype(jnp.float32), weight[:, :, 1].astype(jnp.float32))
        result = jnp.fft.ifft2(spectrum * factor, axes=(0, 1))
        return jnp.stack([jnp.real(result), jnp.imag(result)], axis=2).astype(jnp.bfloat16)

    convolved = lax.map(convolve_slot, (block_of_slot, screened))
    restored = jnp.zeros_like(blocks).at[:, :, :, block_of_slot, :].set(jnp.moveaxis(convolved, 0, 3))
    sigma_new = restored.reshape(NE, NK, 2, NO, NO)
    return sandwich_all(green_ret, sigma_new)
```

```python
import functools

import jax
import jax.numpy as jnp
from jax import lax
from jax.experimental import pallas as pl
from jax.experimental.pallas import tpu as pltpu
from jax.sharding import PartitionSpec as P

import math

AXES = ("energy", "momentum")
LANES = 128
ROWS = 16


def roots(length):
    return [
        (math.cos(2.0 * math.pi * j / length), -math.sin(2.0 * math.pi * j / length))
        for j in range(length)
    ]


def twist(value, phase, length, sign):
    real, imag = value
    phase = phase * sign % length
    if phase == 0:
        return real, imag
    if 4 * phase == length:
        return -imag, real
    if 2 * phase == length:
        return -real, -imag
    if 4 * phase == 3 * length:
        return imag, -real
    if 8 * phase % length == 0:
        half = math.sqrt(0.5)
        if 8 * phase == length:
            return (real - imag) * half, (real + imag) * half
        if 8 * phase == 3 * length:
            return (real + imag) * (-half), (real - imag) * half
        if 8 * phase == 5 * length:
            return (imag - real) * half, (real + imag) * (-half)
        return (real + imag) * half, (imag - real) * half
    angle = 2.0 * math.pi * phase / length
    cosine, sine = math.cos(angle), math.sin(angle)
    return real * cosine - imag * sine, real * sine + imag * cosine


def plus(left, right):
    return left[0] + right[0], left[1] + right[1]


def minus(left, right):
    return left[0] - right[0], left[1] - right[1]


def transform(values, sign):
    length = len(values)
    if length == 1:
        return values
    if length % 2:
        out = []
        for m in range(length):
            total = values[0]
            for e in range(1, length):
                total = plus(total, twist(values[e], m * e % length, length, sign))
            out.append(total)
        return out
    if length == 2:
        return [plus(values[0], values[1]), minus(values[0], values[1])]
    if length % 4 == 0:
        quarter = length // 4
        parts = [transform(values[j::4], sign) for j in range(4)]
        out = [None] * length
        for m in range(quarter):
            a = parts[0][m]
            b = twist(parts[1][m], m, length, sign)
            c = twist(parts[2][m], 2 * m, length, sign)
            d = twist(parts[3][m], 3 * m, length, sign)
            even_plus, even_minus = plus(a, c), minus(a, c)
            odd_plus, odd_minus = plus(b, d), minus(b, d)
            turned = twist(odd_minus, 1, 4, sign)
            out[m] = plus(even_plus, odd_plus)
            out[m + quarter] = plus(even_minus, turned)
            out[m + 2 * quarter] = minus(even_plus, odd_plus)
            out[m + 3 * quarter] = minus(even_minus, turned)
        return out
    half = length // 2
    even = transform(values[0::2], sign)
    odd = transform(values[1::2], sign)
    out = [None] * length
    for m in range(half):
        turned = twist(odd[m], m, length, sign)
        out[m] = plus(even[m], turned)
        out[m + half] = minus(even[m], turned)
    return out


def dot(left, right):
    return jnp.dot(left, right, preferred_element_type=jnp.float32)


def dot_adjoint(left, right):
    return lax.dot_general(left, right, (((1,), (1,)), ((), ())), preferred_element_type=jnp.float32)


def sandwich(green_real, green_imag, sigma_real, sigma_imag):
    first_real = (dot(green_real, sigma_real) - dot(green_imag, sigma_imag)).astype(jnp.bfloat16)
    first_imag = (dot(green_real, sigma_imag) + dot(green_imag, sigma_real)).astype(jnp.bfloat16)
    second_real = dot_adjoint(first_real, green_real) + dot_adjoint(first_imag, green_imag)
    second_imag = dot_adjoint(first_imag, green_real) - dot_adjoint(first_real, green_imag)
    return second_real.astype(jnp.bfloat16), second_imag.astype(jnp.bfloat16)


def opening_kernel(slot_ref, green_ref, sigma_ref, out_ref):
    blocks, rows = out_ref.shape[0], out_ref.shape[4]
    both = sandwich(green_ref[0, 0, 0], green_ref[0, 0, 1], sigma_ref[0, 0, 0], sigma_ref[0, 0, 1])
    for block in range(blocks):
        for part in range(2):
            out_ref[slot_ref[block], 0, 0, part] = both[part][block * rows : (block + 1) * rows]


def closing_kernel(slot_ref, green_ref, packed_ref, out_ref, sigma_ref):
    blocks, rows = packed_ref.shape[0], packed_ref.shape[4]
    for block in range(blocks):
        for part in range(2):
            sigma_ref[part, block * rows : (block + 1) * rows] = packed_ref[slot_ref[block], 0, 0, part]
    both = sandwich(green_ref[0, 0, 0], green_ref[0, 0, 1], sigma_ref[0], sigma_ref[1])
    out_ref[0, 0, 0] = both[0]
    out_ref[0, 0, 1] = both[1]


def convolve_kernel(data_ref, weight_ref, out_ref, work_ref):
    energy_devices, momentum_devices, energies_here, momenta_here = data_ref.shape[:4]
    energies = energy_devices * energies_here
    momenta = momentum_devices * momenta_here
    factor = 1.0 / (energies * momenta)
    halves = data_ref.shape[5] // 8

    def over_half(half, carry):
        rows = pl.ds(pl.multiple_of(half * 8, 8), 8)

        def forward_energy(k, carry):
            device, here = k // momenta_here, k % momenta_here
            values = [
                tuple(
                    data_ref[e // energies_here, device, e % energies_here, here, part, rows].astype(jnp.float32)
                    for part in range(2)
                )
                for e in range(energies)
            ]
            for m, (real, imag) in enumerate(transform(values, -1)):
                work_ref[m, k, 0] = real
                work_ref[m, k, 1] = imag
            return carry

        def momentum_both(m, carry):
            values = [(work_ref[m, k, 0], work_ref[m, k, 1]) for k in range(momenta)]
            product = []
            for n, (real, imag) in enumerate(transform(values, -1)):
                weight_real = weight_ref[m, n, 0, rows].astype(jnp.float32) * factor
                weight_imag = weight_ref[m, n, 1, rows].astype(jnp.float32) * factor
                product.append((real * weight_real - imag * weight_imag, real * weight_imag + imag * weight_real))
            for k, (real, imag) in enumerate(transform(product, 1)):
                work_ref[m, k, 0] = real
                work_ref[m, k, 1] = imag
            return carry

        def inverse_energy(k, carry):
            device, here = k // momenta_here, k % momenta_here
            values = [(work_ref[m, k, 0], work_ref[m, k, 1]) for m in range(energies)]
            for e, value in enumerate(transform(values, 1)):
                for part in range(2):
                    out_ref[e // energies_here, device, e % energies_here, here, part, rows] = value[part].astype(
                        jnp.bfloat16
                    )
            return carry

        lax.fori_loop(0, momenta, forward_energy, 0)
        lax.fori_loop(0, energies, momentum_both, 0)
        lax.fori_loop(0, momenta, inverse_energy, 0)
        return carry

    lax.fori_loop(0, halves, over_half, 0)


def local(green_ret, sigma_in, screened, block_of_slot):
    energies_here, momenta_here, _, orbitals, _ = green_ret.shape
    energy_count = lax.axis_size("energy")
    momentum_count = lax.axis_size("momentum")
    block_count = energy_count * momentum_count
    all_energies = energies_here * energy_count
    all_momenta = momenta_here * momentum_count
    rows = orbitals // block_count
    slot_of_block = (
        jnp.zeros((block_count,), jnp.int32).at[block_of_slot].set(jnp.arange(block_count, dtype=jnp.int32))
    )
    point_spec = pl.BlockSpec((1, 1, 2, orbitals, orbitals), lambda i, j, s: (i, j, 0, 0, 0))
    packed_shape = (block_count, energies_here, momenta_here, 2, rows, orbitals)
    packed_spec = pl.BlockSpec((block_count, 1, 1, 2, rows, orbitals), lambda i, j, s: (0, i, j, 0, 0, 0))
    params = pltpu.CompilerParams(vmem_limit_bytes=60 << 20)

    packed = pl.pallas_call(
        opening_kernel,
        out_shape=jax.ShapeDtypeStruct(packed_shape, jnp.bfloat16),
        grid_spec=pltpu.PrefetchScalarGridSpec(
            num_scalar_prefetch=1,
            grid=(energies_here, momenta_here),
            in_specs=[point_spec, point_spec],
            out_specs=packed_spec,
        ),
        compiler_params=params,
        name="opening",
    )(slot_of_block, green_ret, sigma_in)

    arrived = lax.all_to_all(packed, AXES, split_axis=0, concat_axis=0, tiled=True)

    weight = screened[0]
    data = arrived.reshape(energy_count, momentum_count, energies_here, momenta_here, 2, rows, orbitals)
    high, wide = rows, orbitals
    if rows % ROWS:
        high, wide = ROWS, rows * orbitals // ROWS
        data = data.reshape(*data.shape[:5], high, wide)
    weight = weight.reshape(all_energies, all_momenta, 2, high, wide)
    data_spec = pl.BlockSpec(
        (energy_count, momentum_count, energies_here, momenta_here, 2, high, LANES), lambda i: (0, 0, 0, 0, 0, 0, i)
    )
    outgoing = pl.pallas_call(
        convolve_kernel,
        out_shape=jax.ShapeDtypeStruct(data.shape, jnp.bfloat16),
        grid=(wide // LANES,),
        in_specs=[
            data_spec,
            pl.BlockSpec((all_energies, all_momenta, 2, high, LANES), lambda i: (0, 0, 0, 0, i)),
        ],
        out_specs=data_spec,
        scratch_shapes=[pltpu.VMEM((all_energies, all_momenta, 2, 8, LANES), jnp.float32)],
        compiler_params=params,
        name="convolve",
    )(data, weight)
    outgoing = outgoing.reshape(packed_shape)

    received = lax.all_to_all(outgoing, AXES, split_axis=0, concat_axis=0, tiled=True)

    return pl.pallas_call(
        closing_kernel,
        out_shape=jax.ShapeDtypeStruct(green_ret.shape, jnp.bfloat16),
        grid_spec=pltpu.PrefetchScalarGridSpec(
            num_scalar_prefetch=1,
            grid=(energies_here, momenta_here),
            in_specs=[point_spec, packed_spec],
            out_specs=point_spec,
            scratch_shapes=[pltpu.VMEM((2, orbitals, orbitals), jnp.bfloat16)],
        ),
        compiler_params=params,
        name="closing",
    )(slot_of_block, green_ret, received)


def solution(mesh):
    in_specs = (
        P("energy", "momentum", None, None, None),
        P("energy", "momentum", None, None, None),
        P(("energy", "momentum"), None, None, None, None),
        P(),
    )
    out_specs = P("energy", "momentum", None, None, None)
    return jax.shard_map(local, mesh=mesh, in_specs=in_specs, out_specs=out_specs, check_vma=False)
```

```python
import functools

import jax
import jax.numpy as jnp
from jax import lax
from jax.experimental import pallas as pl
from jax.experimental.pallas import tpu as pltpu
from jax.sharding import PartitionSpec as P

import math

AXES = ("energy", "momentum")
LANES = 128


def twist(value, phase, length, sign):
    real, imag = value
    phase = phase * sign % length
    if phase == 0:
        return real, imag
    if 4 * phase == length:
        return -imag, real
    if 2 * phase == length:
        return -real, -imag
    if 4 * phase == 3 * length:
        return imag, -real
    if 8 * phase % length == 0:
        half = math.sqrt(0.5)
        if 8 * phase == length:
            return (real - imag) * half, (real + imag) * half
        if 8 * phase == 3 * length:
            return (real + imag) * (-half), (real - imag) * half
        if 8 * phase == 5 * length:
            return (imag - real) * half, (real + imag) * (-half)
        return (real + imag) * half, (imag - real) * half
    angle = 2.0 * math.pi * phase / length
    cosine, sine = math.cos(angle), math.sin(angle)
    return real * cosine - imag * sine, real * sine + imag * cosine


def plus(left, right):
    return left[0] + right[0], left[1] + right[1]


def minus(left, right):
    return left[0] - right[0], left[1] - right[1]


def transform(values, sign):
    length = len(values)
    if length == 1:
        return values
    if length % 2:
        out = []
        for m in range(length):
            total = values[0]
            for e in range(1, length):
                total = plus(total, twist(values[e], m * e % length, length, sign))
            out.append(total)
        return out
    if length == 2:
        return [plus(values[0], values[1]), minus(values[0], values[1])]
    if length % 4 == 0:
        quarter = length // 4
        parts = [transform(values[j::4], sign) for j in range(4)]
        out = [None] * length
        for m in range(quarter):
            a = parts[0][m]
            b = twist(parts[1][m], m, length, sign)
            c = twist(parts[2][m], 2 * m, length, sign)
            d = twist(parts[3][m], 3 * m, length, sign)
            even_plus, even_minus = plus(a, c), minus(a, c)
            odd_plus, odd_minus = plus(b, d), minus(b, d)
            turned = twist(odd_minus, 1, 4, sign)
            out[m] = plus(even_plus, odd_plus)
            out[m + quarter] = plus(even_minus, turned)
            out[m + 2 * quarter] = minus(even_plus, odd_plus)
            out[m + 3 * quarter] = minus(even_minus, turned)
        return out
    half = length // 2
    even = transform(values[0::2], sign)
    odd = transform(values[1::2], sign)
    out = [None] * length
    for m in range(half):
        turned = twist(odd[m], m, length, sign)
        out[m] = plus(even[m], turned)
        out[m + half] = minus(even[m], turned)
    return out


def dot(left, right):
    return jnp.dot(left, right, preferred_element_type=jnp.float32)


def dot_adjoint(left, right):
    return lax.dot_general(left, right, (((1,), (1,)), ((), ())), preferred_element_type=jnp.float32)


def inner_count(energy_count):
    return 2 if energy_count % 2 == 0 else 1


def towards(index, step, count):
    return index ^ step if count & (count - 1) == 0 else (index + step) % count


def back_from(index, step, count):
    return index ^ step if count & (count - 1) == 0 else (index + count - step) % count


def place():
    energy = lax.axis_index("energy")
    momentum = lax.axis_index("momentum")
    cores = inner_count(lax.axis_size("energy"))
    return energy // cores, energy % cores * lax.axis_size("momentum") + momentum


def opening_kernel(fresh, row_half, rows, *refs):
    if fresh:
        order_ref, green_ref, sigma_ref, column_ref = refs[:4]
        outs, first_ref, picked_ref, stage_ref = refs[4:-3], refs[-3], refs[-2], refs[-1]
    else:
        order_ref, first_ref, column_ref = refs[:3]
        outs, stage_ref = refs[3:-1], refs[-1]
    layers, plane = len(outs), outs[0].shape[0]
    layer, _ = place()
    part_rows = outs[0].shape[4]
    blocks = layers * plane
    if fresh:
        for part in range(2):
            for block in range(blocks):
                start = block * rows + row_half * part_rows
                picked_ref[part, block * part_rows : (block + 1) * part_rows] = green_ref[
                    0, 0, part, start : start + part_rows
                ]
        first_ref[0, 0, 0] = (
            dot(picked_ref[0], sigma_ref[0, 0, 0]) - dot(picked_ref[1], sigma_ref[0, 0, 1])
        ).astype(jnp.bfloat16)
        first_ref[0, 0, 1] = (
            dot(picked_ref[0], sigma_ref[0, 0, 1]) + dot(picked_ref[1], sigma_ref[0, 0, 0])
        ).astype(jnp.bfloat16)
    first_real, first_imag = first_ref[0, 0, 0], first_ref[0, 0, 1]
    column_real, column_imag = column_ref[0, 0, 0], column_ref[0, 0, 1]
    both = (
        (dot_adjoint(first_real, column_real) + dot_adjoint(first_imag, column_imag)).astype(jnp.bfloat16),
        (dot_adjoint(first_imag, column_real) - dot_adjoint(first_real, column_imag)).astype(jnp.bfloat16),
    )
    for part in range(2):
        for block in range(blocks):
            stage_ref[block, part] = both[part][block * part_rows : (block + 1) * part_rows]
    for step in range(layers):
        for seat in range(plane):
            slot = towards(layer, step, layers) * plane + seat
            outs[step][seat, 0, 0] = stage_ref[order_ref[slot]]


def spread_kernel(layers, plane, *refs):
    ins, outs = refs[:layers], refs[layers:]
    _, seat = place()
    for turn in range(plane):
        for step in range(layers):
            outs[turn][step] = ins[step][towards(seat, turn, plane)]


def collect_kernel(layers, plane, *refs):
    ins, outs = refs[:plane], refs[plane:]
    layer, _ = place()
    for step in range(layers):
        for turn in range(plane):
            outs[step][turn] = ins[turn][towards(layer, step, layers)]


def convolve_kernel(momentum_count, *refs):
    work_ref, data_ref = refs[-1], refs[-2]
    plane = (len(refs) - 3) // 2
    ins, weight_ref, outs = refs[:plane], refs[plane], refs[plane + 1 : 2 * plane + 1]
    layers, energies_here, momenta_here = ins[0].shape[:3]
    cores = plane // momentum_count
    layer, seat = place()
    energies = layers * cores * energies_here
    momenta = momentum_count * momenta_here
    factor = 1.0 / (energies * momenta)
    for turn in range(plane):
        for step in range(layers):
            data_ref[back_from(seat, turn, plane), back_from(layer, step, layers)] = ins[turn][step]

    def spot(e, device):
        source = e // energies_here
        return source % cores * momentum_count + device, source // cores, e % energies_here

    def forward_energy(k, carry):
        device, here = k // momenta_here, k % momenta_here
        values = []
        for e in range(energies):
            a, b, c = spot(e, device)
            values.append(tuple(data_ref[a, b, c, here, part].astype(jnp.float32) for part in range(2)))
        for m, (real, imag) in enumerate(transform(values, -1)):
            work_ref[m, k, 0] = real
            work_ref[m, k, 1] = imag
        return carry

    def momentum_both(m, carry):
        values = [(work_ref[m, k, 0], work_ref[m, k, 1]) for k in range(momenta)]
        product = []
        for n, (real, imag) in enumerate(transform(values, -1)):
            weight_real = weight_ref[m, n, 0].astype(jnp.float32) * factor
            weight_imag = weight_ref[m, n, 1].astype(jnp.float32) * factor
            product.append((real * weight_real - imag * weight_imag, real * weight_imag + imag * weight_real))
        for k, (real, imag) in enumerate(transform(product, 1)):
            work_ref[m, k, 0] = real
            work_ref[m, k, 1] = imag
        return carry

    def inverse_energy(k, carry):
        device, here = k // momenta_here, k % momenta_here
        values = [(work_ref[m, k, 0], work_ref[m, k, 1]) for m in range(energies)]
        for e, value in enumerate(transform(values, 1)):
            a, b, c = spot(e, device)
            for part in range(2):
                data_ref[a, b, c, here, part] = value[part].astype(jnp.bfloat16)
        return carry

    lax.fori_loop(0, momenta, forward_energy, 0)
    lax.fori_loop(0, energies, momentum_both, 0)
    lax.fori_loop(0, momenta, inverse_energy, 0)
    for turn in range(plane):
        outs[turn][...] = data_ref[towards(seat, turn, plane)]


def closing_kernel(row_parts, layers, rows, last, *refs):
    order_ref, green_ref, column_ref = refs[:3]
    ins = refs[3 : 3 + row_parts * layers]
    rest = refs[3 + row_parts * layers :]
    total_ref = rest[0] if last else None
    out_ref, stage_ref, sigma_ref = rest[-3], rest[-2], rest[-1]
    plane, part_rows = ins[0].shape[0], ins[0].shape[4]
    layer, seat = place()
    blocks = layers * plane
    for row_half in range(row_parts):
        for step in range(layers):
            for turn in range(plane):
                slot = back_from(layer, step, layers) * plane + back_from(seat, turn, plane)
                stage_ref[order_ref[slot], row_half] = ins[row_half * layers + step][turn, 0, 0]
    for part in range(2):
        for block in range(blocks):
            for row_half in range(row_parts):
                start = block * rows + row_half * part_rows
                sigma_ref[part, start : start + part_rows] = stage_ref[block, row_half, part]
    green_real, green_imag = green_ref[0, 0, 0], green_ref[0, 0, 1]
    first_real = (dot(green_real, sigma_ref[0]) - dot(green_imag, sigma_ref[1])).astype(jnp.bfloat16)
    first_imag = (dot(green_real, sigma_ref[1]) + dot(green_imag, sigma_ref[0])).astype(jnp.bfloat16)
    column_real, column_imag = column_ref[0, 0, 0], column_ref[0, 0, 1]
    second_real = dot_adjoint(first_real, column_real) + dot_adjoint(first_imag, column_imag)
    second_imag = dot_adjoint(first_imag, column_real) - dot_adjoint(first_real, column_imag)
    if last:
        second_real += total_ref[0, 0, 0]
        second_imag += total_ref[0, 0, 1]
    out_ref[0, 0, 0] = second_real.astype(out_ref.dtype)
    out_ref[0, 0, 1] = second_imag.astype(out_ref.dtype)


def local(green_ret, sigma_in, screened, block_of_slot):
    energies_here, momenta_here, _, orbitals, _ = green_ret.shape
    energy_count = lax.axis_size("energy")
    momentum_count = lax.axis_size("momentum")
    block_count = energy_count * momentum_count
    all_energies = energies_here * energy_count
    all_momenta = momenta_here * momentum_count
    cores = inner_count(energy_count)
    layers, plane = energy_count // cores, cores * momentum_count
    rows = orbitals // block_count
    row_parts, column_parts = parts_of(rows)
    part_rows, width = rows // row_parts, orbitals // column_parts
    grid = (energies_here, momenta_here)

    def params(mebibytes):
        return pltpu.CompilerParams(vmem_limit_bytes=mebibytes << 20)

    bf16 = jnp.bfloat16

    point_spec = pl.BlockSpec((1, 1, 2, orbitals, orbitals), lambda i, j, s: (i, j, 0, 0, 0))
    piece = (energies_here, momenta_here, 2, part_rows, width)
    seat_shape = jax.ShapeDtypeStruct((plane, *piece), bf16)
    seat_spec = pl.BlockSpec((plane, 1, 1, 2, part_rows, width), lambda i, j, s: (0, i, j, 0, 0, 0))
    layer_shape = jax.ShapeDtypeStruct((layers, *piece), bf16)
    first_shape = jax.ShapeDtypeStruct((energies_here, momenta_here, 2, orbitals // row_parts, orbitals), bf16)
    first_spec = pl.BlockSpec((1, 1, 2, orbitals // row_parts, orbitals), lambda i, j, s: (i, j, 0, 0, 0))
    stage = pltpu.VMEM((block_count, 2, part_rows, width), bf16)

    def column_rows(column):
        return pl.BlockSpec((1, 1, 2, width, orbitals), lambda i, j, s: (i, j, 0, column, 0))

    def columns(column):
        return pl.BlockSpec((1, 1, 2, orbitals, width), lambda i, j, s: (i, j, 0, 0, column))

    def opening(row_half, column, source):
        fresh = column == 0
        return pl.pallas_call(
            functools.partial(opening_kernel, fresh, row_half, rows),
            out_shape=(seat_shape,) * layers + ((first_shape,) if fresh else ()),
            grid_spec=pltpu.PrefetchScalarGridSpec(
                num_scalar_prefetch=1,
                grid=grid,
                in_specs=[point_spec, point_spec, column_rows(column)]
                if fresh
                else [first_spec, column_rows(column)],
                out_specs=(seat_spec,) * layers + ((first_spec,) if fresh else ()),
                scratch_shapes=([pltpu.VMEM((2, orbitals // row_parts, orbitals), bf16)] if fresh else []) + [stage],
            ),
            compiler_params=params(16),
        )(block_of_slot, *source, green_ret)

    def hops(buffers, count, pairs):
        moved = [buffers[0]]
        for step in range(1, count):
            moved.append(lax.ppermute(buffers[step], AXES, pairs(step)))
        return moved

    def layer_pairs(step):
        return [
            (z * plane + q, towards(z, step, layers) * plane + q) for z in range(layers) for q in range(plane)
        ]

    def plane_pairs(step):
        return [
            (z * plane + q, z * plane + towards(q, step, plane)) for z in range(layers) for q in range(plane)
        ]

    def reorder(kernel, buffers, count, shape):
        spec = pl.BlockSpec(memory_space=pltpu.VMEM)
        return pl.pallas_call(
            functools.partial(kernel, layers, plane),
            out_shape=(shape,) * count,
            in_specs=[spec] * len(buffers),
            out_specs=(spec,) * count,
            compiler_params=params(4),
        )(*buffers)

    weight = screened[0].reshape(all_energies, all_momenta, 2, rows, orbitals)

    def convolve(row_half, column, buffers):
        piece_spec = pl.BlockSpec(
            (layers, energies_here, momenta_here, 2, part_rows, LANES), lambda i: (0, 0, 0, 0, 0, i)
        )
        base = column * (width // LANES)
        return pl.pallas_call(
            functools.partial(convolve_kernel, momentum_count),
            out_shape=(layer_shape,) * plane,
            grid=(width // LANES,),
            in_specs=[piece_spec] * plane
            + [
                pl.BlockSpec(
                    (all_energies, all_momenta, 2, part_rows, LANES), lambda i: (0, 0, 0, row_half, base + i)
                )
            ],
            out_specs=(piece_spec,) * plane,
            scratch_shapes=[
                pltpu.VMEM((plane, layers, energies_here, momenta_here, 2, part_rows, LANES), bf16),
                pltpu.VMEM((all_energies, all_momenta, 2, part_rows, LANES), jnp.float32),
            ],
            compiler_params=params(12),
        )(*buffers, weight)

    def closing(column, buffers, total):
        last = total is not None
        total_shape = jax.ShapeDtypeStruct(green_ret.shape, jnp.float32)
        return pl.pallas_call(
            functools.partial(closing_kernel, row_parts, layers, rows, last),
            out_shape=jax.ShapeDtypeStruct(green_ret.shape, bf16) if last else total_shape,
            grid_spec=pltpu.PrefetchScalarGridSpec(
                num_scalar_prefetch=1,
                grid=grid,
                in_specs=[point_spec, columns(column)]
                + [seat_spec] * len(buffers)
                + ([point_spec] if last else []),
                out_specs=point_spec,
                scratch_shapes=[
                    pltpu.VMEM((block_count, row_parts, 2, part_rows, width), bf16),
                    pltpu.VMEM((2, orbitals, width), bf16),
                ],
            ),
            compiler_params=params(20),
        )(block_of_slot, green_ret, green_ret, *buffers, *((total,) if last else ()))

    firsts, arrived = {}, {}
    chunks = [(row_half, column) for column in range(column_parts) for row_half in range(row_parts)]
    opened = {}
    for row_half, column in chunks:
        if column == 0:
            *outs, firsts[row_half] = opening(row_half, column, (green_ret, sigma_in))
        else:
            outs = opening(row_half, column, (firsts[row_half],))
        opened[row_half, column] = outs
    for row_half, column in chunks:
        crossed = hops(opened[row_half, column], layers, layer_pairs)
        packed = reorder(spread_kernel, crossed, plane, layer_shape)
        spread = hops(packed, plane, plane_pairs)
        convolved = convolve(row_half, column, spread)
        returned = hops(convolved, plane, plane_pairs)
        packed = reorder(collect_kernel, returned, layers, seat_shape)
        arrived[row_half, column] = hops(packed, layers, layer_pairs)
    total = None
    for column in range(column_parts):
        buffers = [b for row_half in range(row_parts) for b in arrived[row_half, column]]
        total = closing(column, buffers, total)
    return total


def parts_of(rows):
    return (2 if rows % 16 == 0 else 1), 2


def solution(mesh):
    in_specs = (
        P("energy", "momentum", None, None, None),
        P("energy", "momentum", None, None, None),
        P(("energy", "momentum"), None, None, None, None),
        P(),
    )
    out_specs = P("energy", "momentum", None, None, None)
    return jax.shard_map(local, mesh=mesh, in_specs=in_specs, out_specs=out_specs, check_vma=False)
```
